32 devices in a mesh: ens: 4 (over x, core), space: 8 (over z, y).
Axes of the slice: x: 2, y: 2, z: 4, core: 2. Of those that a mesh axis runs over, the one named last changes fastest.
Arguments:
- latents: bfloat16 [8, 32, 256, 256], P('ens', None, 'space'), may hold values from -6 to 6
- targets: bfloat16 [32, 256, 256], P(None, 'space'), may hold values from -6 to 6
- kernel: bfloat16 [3, 3, 256, 256], replicated, may hold values from -0.125 to 0.125
Outputs:
- loss: float32 [], replicated
- grad_input: bfloat16 [8, 32, 256, 256], P('ens', None, 'space')
- grad_kernel: float32 [3, 3, 256, 256], replicated
The draws below stay inside these ranges and needn't reach their ends.
All inputs are finite; a program needn't handle non-finite values.
Results may differ from the reference program's by a relative error of at most 0.0047.
Values may be sent and summed in bfloat16 or wider, within the bound.
A program may use at most 64 MiB of HBM per device.

```python
import jax
import jax.numpy as jnp
from jax import lax

C = 256
MEMBERS = 8
ROWS = 32
LON = 256


def level_of(stream_key, extent, split, smallest, high):
    factor_of = 1.0
    for position, blocks in split:
        steps = jax.random.uniform(jax.random.fold_in(jax.random.fold_in(stream_key, 6), position), (blocks,), jnp.float32, smallest / len(split), high / len(split))
        factor_of = factor_of * jnp.repeat(jnp.exp(steps), extent[position] // blocks).reshape((-1,) + (1,) * (len(extent) - 1 - position))
    return factor_of


def gaussian(rng, shape, scale, reach, shards=(), kind=jnp.bfloat16):
    result = jax.random.normal(rng, shape, jnp.float32) * scale
    if len(shards) > 0:
        result = level_of(rng, shape, shards, -0.22, 0.18) * result
    return jnp.clip(result, min=-reach, max=reach).astype(kind)


def setup_inputs(seed: int = 0) -> dict:
    key_of = jax.random.split(jax.random.key(seed), 4)
    latents = gaussian(key_of[0], (MEMBERS, ROWS, LON, C), 1.0, 6.0, ((0, 4), (2, 8)))
    targets = gaussian(key_of[1], (ROWS, LON, C), 1.0, 6.0, ((1, 8),))
    kernel = gaussian(key_of[2], (3, 3, C, C), (9 * C) ** -0.5, 0.125)
    return dict(latents=latents, targets=targets, kernel=kernel)


smoothing = 0.1

def border(field):
    wrapped = jnp.concatenate([field[:, :, -1:], field, field[:, :, :1]], axis=2)
    return jnp.pad(wrapped, ((0, 0), (1, 1), (0, 0), (0, 0)))

def conv_forward(padded, kernel, rows, cols):
    chans = padded.shape[3]
    total = None
    for row_off in range(3):
        for col_off in range(3):
            window = padded[:, row_off:row_off + rows, col_off:col_off + cols, :].reshape(-1, chans)
            term = jnp.dot(window, kernel[row_off, col_off], preferred_element_type=jnp.float32)
            total = term if total is None else total + term
    return total.reshape(padded.shape[0], rows, cols, -1)

def conv_adjoint(padded, kernel, rows, cols):
    chans = padded.shape[3]
    total = None
    for row_off in range(3):
        for col_off in range(3):
            window = padded[:, 2 - row_off:2 - row_off + rows, 2 - col_off:2 - col_off + cols, :].reshape(-1, chans)
            term = lax.dot_general(window, kernel[row_off, col_off], (((1,), (1,)), ((), ())), preferred_element_type=jnp.float32)
            total = term if total is None else total + term
    return total.reshape(padded.shape[0], rows, cols, -1)

def kernel_terms(padded, slopes, rows, cols):
    chans = padded.shape[3]
    flat_slopes = slopes.reshape(-1, slopes.shape[3])
    blocks = []
    for row_off in range(3):
        for col_off in range(3):
            window = padded[:, row_off:row_off + rows, col_off:col_off + cols, :].reshape(-1, chans)
            blocks.append(lax.dot_general(window, flat_slopes, (((0,), (0,)), ((), ())), preferred_element_type=jnp.float32))
    return jnp.stack(blocks).reshape(3, 3, chans, -1)

def reference(latents, targets, kernel):
    members, rows, cols, chans = latents.shape
    padded = border(latents)
    fields = conv_forward(padded, kernel, rows, cols)
    offset = fields - targets.astype(jnp.float32)[None]
    spread = jnp.sqrt(offset * offset + smoothing * smoothing)
    own_total = jnp.sum(spread)
    own_slope = offset / spread
    pair_total = jnp.zeros((), jnp.float32)
    slope_rows = []
    for member in range(members):
        accum = jnp.zeros(fields.shape[1:], jnp.float32)
        for other in range(members):
            if other != member:
                gap = fields[member] - fields[other]
                width = jnp.sqrt(gap * gap + smoothing * smoothing)
                pair_total = pair_total + jnp.sum(width)
                accum = accum + gap / width
        slope_rows.append(accum)
    pair_slope = jnp.stack(slope_rows)
    total = own_total / members - pair_total / (2 * members * (members - 1))
    loss = total / (rows * cols * chans)
    slopes = (own_slope / members - pair_slope / (members * (members - 1))).astype(jnp.bfloat16)
    grad_input = conv_adjoint(border(slopes), kernel, rows, cols).astype(jnp.bfloat16)
    grad_kernel = kernel_terms(padded, slopes, rows, cols) / (members * rows * cols)
    return (loss, grad_input, grad_kernel)
```

```python
import functools

import jax
import jax.numpy as jnp
from jax import lax
from jax.experimental import pallas as pl
from jax.experimental.pallas import tpu as pltpu
from jax.sharding import PartitionSpec as P

smoothing = 0.1
WIRE = jnp.bfloat16
ROW_CHUNK = 4
F32, BF16 = jnp.float32, jnp.bfloat16
NT = (((1,), (1,)), ((), ()))


def rim(block, count):
    cols = block.shape[2]
    forward = [(i, (i + 1) % count) for i in range(count)]
    backward = [(t, s) for s, t in forward]
    low = lax.ppermute(block[:, :, cols - 1 :], "space", forward)
    high = lax.ppermute(block[:, :, :1], "space", backward)
    left = jnp.concatenate([low, block[:, :, : cols - 1]], axis=2)
    right = jnp.concatenate([block[:, :, 1:], high], axis=2)
    return jnp.pad(jnp.stack([left, block, right]), ((0, 0), (0, 0), (1, 1), (0, 0), (0, 0)))


def body(
    n, members,
    x_ref, t_ref, k_ref,
    gi_ref, gk_ref, loss_ref,
    f_own, own, co, xp, xc, sp, acc, eo, ei, r1, b2, r2, b3, r3, l1, lr1, l2, lr2, l3, lr3,
    s_x, r_x, s_c, r_c, s_l, r_l, s_e, r_e, s_st, r_st, s_ls, r_ls, s_sp, r_sp, s_lp, r_lp,
    s_ag, r_ag,
):
    mdev, rows, cols, chans = gi_ref.shape
    rc = ROW_CHUNK
    chunks = rows // rc
    cells = rc * cols
    part = b3.shape[0] // n
    e = lax.axis_index("ens")
    s = lax.axis_index("space")
    core = lax.rem(e, 2)
    xx = e // 2
    cpeer = {"ens": xx * 2 + (1 - core)}
    xpeer = {"ens": (1 - xx) * 2 + core}
    right = {"space": lax.rem(s + 1, n)}
    left = {"space": lax.rem(s + n - 1, n)}

    def rcopy(src, dst, ss, rs, dev):
        return pltpu.make_async_remote_copy(
            src_ref=src, dst_ref=dst, send_sem=ss, recv_sem=rs,
            device_id=dev, device_id_type=pl.DeviceIdType.MESH,
        )

    barrier = pltpu.get_barrier_semaphore()
    for dev in (cpeer, xpeer):
        pl.semaphore_signal(barrier, inc=1, device_id=dev, device_id_type=pl.DeviceIdType.MESH)

    @pl.loop(1, n)
    def _(d):
        pl.semaphore_signal(
            barrier, inc=1, device_id={"space": lax.rem(s + d, n)},
            device_id_type=pl.DeviceIdType.MESH,
        )

    pl.semaphore_wait(barrier, n + 1)

    def to_x(ch):
        return rcopy(own.at[ch], xp.at[ch], s_x.at[ch], r_x.at[ch], xpeer)

    def to_core(ch):
        return rcopy(own.at[ch], co.at[ch], s_c.at[ch], r_c.at[ch], cpeer)

    def relay(ch):
        return rcopy(xp.at[ch], xc.at[ch], s_l.at[ch], r_l.at[ch], cpeer)

    @pl.loop(0, chunks)
    def _(ch):
        total = None
        for a in range(3):
            for b in range(3):
                w = x_ref[b, :, pl.ds(ch * rc + a, rc)].reshape(mdev * cells, chans)
                term = jnp.dot(w, k_ref[a * 3 + b], preferred_element_type=F32)
                total = term if total is None else total + term
        total = total.reshape(mdev, cells, chans)
        f_own[ch] = total
        own[ch] = total.astype(WIRE)
        to_x(ch).start()
        to_core(ch).start()

    acc[...] = jnp.zeros_like(acc)
    loss_ref[...] = jnp.zeros_like(loss_ref)
    for c in range(3):
        for r in (0, rows + 1):
            sp[c, :, r] = jnp.zeros((mdev, cols, chans), BF16)

    def smooth(gap):
        square = gap * gap + smoothing * smoothing
        inv = lax.rsqrt(square)
        return gap * inv, square * inv

    def process(ch):
        @pl.loop(0, rc)
        def _(q):
            row = ch * rc + q
            for blk in range(cols // 16):
                at = pl.ds(pl.multiple_of(q * cols + blk * 16, 16), 16)
                mine = [f_own[ch, m, at] for m in range(mdev)]
                tgt = t_ref[row, pl.ds(blk * 16, 16)].astype(F32)
                slopes, own_w, pair_w = [], None, None
                own_s = []
                for f in mine:
                    sl, w = smooth(f - tgt)
                    own_s.append(sl)
                    own_w = w if own_w is None else own_w + w
                sl, w = smooth(mine[0] - mine[1])
                sums = [sl, -sl]
                pair_w = w + w
                for ref in (co, xp, xc):
                    for m in range(mdev):
                        o = ref[ch, m, at].astype(F32)
                        for k in range(mdev):
                            sl, w = smooth(mine[k] - o)
                            sums[k] = sums[k] + sl
                            pair_w = pair_w + w
                loss_ref[...] += own_w * (1.0 / members) - pair_w * (
                    1.0 / (2 * members * (members - 1))
                )
                for m in range(mdev):
                    sl = own_s[m] * (1.0 / members) - sums[m] * (1.0 / (members * (members - 1)))
                    sp[1, m, 1 + row, pl.ds(blk * 16, 16)] = sl.astype(BF16)
                    if blk == 0:
                        eo[0, pl.ds(m * rows + row, 1)] = sl[0:1]
                    if blk == cols // 16 - 1:
                        eo[1, pl.ds(m * rows + row, 1)] = sl[15:16]

        sl = sp[1, :, pl.ds(1 + ch * rc, rc)].reshape(mdev * cells, chans)
        slt = sl.astype(F32).T.astype(BF16)
        for tap in range(9):
            a, b = tap // 3, tap % 3
            w = x_ref[b, :, pl.ds(ch * rc + a, rc)].reshape(mdev * cells, chans)
            p = jnp.dot(slt, w, preferred_element_type=F32)
            for dh in range(2):
                piece = tap * 2 + dh
                xh, off = piece // 9, (piece % 9) * 128
                for h in range(2):
                    acc[h, xh, off : off + 128] += p[
                        dh * 128 : dh * 128 + 128, h * 128 : h * 128 + 128
                    ]

    to_x(0).wait_recv()
    relay(0).start()

    @pl.loop(0, chunks)
    def _(ch):
        @pl.when(ch + 1 < chunks)
        def _():
            to_x(ch + 1).wait_recv()
            relay(ch + 1).start()

        to_core(ch).wait_recv()
        relay(ch).wait_recv()
        process(ch)

    edges = [
        rcopy(eo.at[1], ei.at[0], s_e.at[0], r_e.at[0], right),
        rcopy(eo.at[0], ei.at[1], s_e.at[1], r_e.at[1], left),
    ]
    for c in edges:
        c.start()
    st_core = rcopy(acc.at[1 - core], r1, s_st.at[0], r_st.at[0], cpeer)
    st_core.start()
    total = loss_ref[...]
    total = total[0:8, 0:128] + total[8:16, 0:128] + total[0:8, 128:256] + total[8:16, 128:256]
    l1[...] = total
    ls_core = rcopy(l1, lr1, s_ls.at[0], r_ls.at[0], cpeer)
    ls_core.start()

    for c in edges:
        c.wait_recv()
    col = lax.broadcasted_iota(jnp.int32, (cols, chans), 0)

    @pl.loop(0, mdev * rows)
    def _(i):
        m, row = i // rows, lax.rem(i, rows)
        v = sp[1, m, 1 + row].astype(F32)
        lo = jnp.where(col == 0, ei[0, pl.ds(i, 1)], pltpu.roll(v, 1, 0))
        hi = jnp.where(col == cols - 1, ei[1, pl.ds(i, 1)], pltpu.roll(v, cols - 1, 0))
        sp[0, m, 1 + row] = lo.astype(BF16)
        sp[2, m, 1 + row] = hi.astype(BF16)

    def grad_in(start, stop):
        @pl.loop(start, stop)
        def _(ch):
            total = None
            for a in range(3):
                for b in range(3):
                    w = sp[2 - b, :, pl.ds(ch * rc + 2 - a, rc)].reshape(mdev * cells, chans)
                    term = lax.dot_general(
                        w, k_ref[a * 3 + b], NT, preferred_element_type=F32
                    )
                    total = term if total is None else total + term
            gi_ref[:, pl.ds(ch * rc, rc)] = total.reshape(mdev, rc, cols, chans).astype(BF16)

    ls_core.wait_recv()
    l2[...] = l1[...] + lr1[...]
    ls_x = rcopy(l2, lr2, s_ls.at[1], r_ls.at[1], xpeer)
    ls_x.start()
    st_core.wait_recv()
    b2[...] = (acc[core, 1 - xx] + r1[1 - xx]).astype(BF16)
    st_x = rcopy(b2, r2, s_st.at[1], r_st.at[1], xpeer)
    st_x.start()
    grad_in(0, chunks // 2)

    ls_x.wait_recv()
    l3[...] = l2[...] + lr2[...]
    st_x.wait_recv()
    total = acc[core, xx] + r1[xx] + r2[...].astype(F32)
    r1[xx] = total
    b3[...] = total.astype(BF16)

    def part_of(i):
        return pl.ds(pl.multiple_of(i * part, 16), part)

    def to_strip(d, i):
        peer = lax.rem(s + d, n)
        return rcopy(
            b3.at[part_of(peer)], r3.at[i], s_sp.at[d], r_sp.at[i], {"space": peer}
        ), rcopy(l3, lr3.at[i], s_lp.at[d], r_lp.at[i], {"space": peer})

    @pl.loop(1, n)
    def _(d):
        for c in to_strip(d, s):
            c.start()

    grad_in(chunks // 2, chunks - chunks // 4)

    r2_total = r1[xx, part_of(s)]
    l_total = l3[...]

    def take(d, carry):
        g, l = carry
        peer = lax.rem(s + d, n)
        for c in to_strip(d, peer):
            c.wait_recv()
        return g + r3[peer].astype(F32), l + lr3[peer]

    r2_total, l_total = lax.fori_loop(1, n, take, (r2_total, l_total))
    gk_ref[core, xx, part_of(s)] = r2_total.astype(BF16)

    def gather(d, i):
        return rcopy(
            gk_ref.at[core, xx, part_of(i)], gk_ref.at[core, xx, part_of(i)],
            s_ag.at[d], r_ag.at[i], {"space": lax.rem(s + d, n)},
        )

    @pl.loop(1, n)
    def _(d):
        gather(d, s).start()

    grad_in(chunks - chunks // 4, chunks)
    loss_ref[0:8, 0:128] = l_total

    @pl.loop(1, n)
    def _(d):
        gather(d, lax.rem(s + d, n)).wait_recv()

    ag_x = rcopy(gk_ref.at[core, xx], gk_ref.at[core, xx], s_st.at[2], r_st.at[2], xpeer)
    ag_x.start()
    rcopy(gk_ref.at[core, 1 - xx], gk_ref.at[core, 1 - xx], s_st.at[2], r_st.at[2], xpeer).wait_recv()
    ag_c = rcopy(gk_ref.at[core], gk_ref.at[core], s_st.at[3], r_st.at[3], cpeer)
    ag_c.start()
    rcopy(gk_ref.at[1 - core], gk_ref.at[1 - core], s_st.at[3], r_st.at[3], cpeer).wait_recv()

    @pl.loop(0, chunks)
    def _(ch):
        to_x(ch).wait_send()
        to_core(ch).wait_send()
        relay(ch).wait_send()

    @pl.loop(1, n)
    def _(d):
        for c in to_strip(d, s):
            c.wait_send()
        gather(d, s).wait_send()

    for c in edges + [st_core, ls_core, ls_x, st_x, ag_x, ag_c]:
        c.wait_send()


def local(n, latents, targets, kernel):
    mdev, rows, cols, chans = latents.shape
    members = mdev * 4
    chunks = rows // ROW_CHUNK
    cells = ROW_CHUNK * cols
    x = rim(latents, n)
    part = -(-9 * 128 // (16 * n)) * 16
    hp = part * n
    vmem, dma = pltpu.VMEM, pltpu.SemaphoreType.DMA
    wire = vmem((chunks, mdev, cells, chans), WIRE)
    tile = vmem((8, 128), F32)
    gi, gk, loss = pl.pallas_call(
        functools.partial(body, n, members),
        name="crps_step",
        out_shape=(
            jax.ShapeDtypeStruct(latents.shape, BF16),
            jax.ShapeDtypeStruct((2, 2, hp, 128), BF16),
            jax.ShapeDtypeStruct((16, chans), F32),
        ),
        in_specs=[pl.BlockSpec(memory_space=vmem)] * 3,
        out_specs=(pl.BlockSpec(memory_space=vmem),) * 3,
        scratch_shapes=[
            vmem((chunks, mdev, cells, chans), F32),
            wire, wire, wire, wire,
            vmem((3, mdev, rows + 2, cols, chans), BF16),
            vmem((2, 2, hp, 128), F32),
            vmem((2, mdev * rows, chans), F32),
            vmem((2, mdev * rows, chans), F32),
            vmem((2, hp, 128), F32),
            vmem((hp, 128), BF16),
            vmem((hp, 128), BF16),
            vmem((hp, 128), BF16),
            vmem((n, part, 128), BF16),
            tile, tile, tile, tile, tile,
            vmem((n, 8, 128), F32),
            dma((chunks,)), dma((chunks,)), dma((chunks,)), dma((chunks,)),
            dma((chunks,)), dma((chunks,)),
            dma((2,)), dma((2,)), dma((4,)), dma((4,)), dma((2,)), dma((2,)),
            dma((n,)), dma((n,)), dma((n,)), dma((n,)), dma((n,)), dma((n,)),
        ],
        compiler_params=pltpu.CompilerParams(
            collective_id=0, has_side_effects=True, vmem_limit_bytes=48 * 2**20
        ),
    )(x, targets, kernel.reshape(9, chans, chans))
    longitude = cols * n
    gk = gk[:, :, : 9 * 128].reshape(2, 9, chans, 128).transpose(1, 0, 3, 2)
    grad_kernel = gk.astype(F32).reshape(3, 3, chans, chans) / (members * rows * longitude)
    loss = jnp.sum(loss[0:8, 0:128]) / (rows * longitude * chans)
    return loss, gi, grad_kernel


def solution(mesh):
    in_specs = (P("ens", None, "space", None), P(None, "space", None), P())
    out_specs = (P(), P("ens", None, "space", None), P())
    return jax.shard_map(
        functools.partial(local, mesh.shape["space"]),
        mesh=mesh, in_specs=in_specs, out_specs=out_specs, check_vma=False,
    )
```

```python
import functools

import jax
import jax.numpy as jnp
from jax import lax
from jax.experimental import pallas as pl
from jax.experimental.pallas import tpu as pltpu
from jax.sharding import PartitionSpec as P

smoothing = 0.1
WIRE = jnp.bfloat16
ROW_CHUNK = 4
PIECES = 3
F32, BF16 = jnp.float32, jnp.bfloat16
NT = (((1,), (1,)), ((), ()))


def body(
    n, members,
    lat_ref, t_ref, k_ref,
    gi_ref, gk_ref, loss_ref,
    x_ref, leo, lei, f_own, own, co, xp, xc, sp, acc, eo, ei, r1, b2, r2, b3, r3, l1, lr1, l2, lr2, l3, lr3,
    s_x, r_x, s_c, r_c, s_l, r_l, s_e, r_e, s_st, r_st, s_x2, r_x2, s_ls, r_ls, s_sp, r_sp, s_lp, r_lp,
    s_ag, r_ag, s_le, r_le, s_ax, r_ax, s_ac, r_ac,
):
    mdev, rows, cols, chans = gi_ref.shape
    rc = ROW_CHUNK
    chunks = rows // rc
    cells = rc * cols
    part = b3.shape[0] // (n * PIECES)
    span = part * n
    e = lax.axis_index("ens")
    s = lax.axis_index("space")
    core = lax.rem(e, 2)
    xx = e // 2
    cpeer = {"ens": xx * 2 + (1 - core)}
    xpeer = {"ens": (1 - xx) * 2 + core}
    right = {"space": lax.rem(s + 1, n)}
    left = {"space": lax.rem(s + n - 1, n)}

    def rcopy(src, dst, ss, rs, dev):
        return pltpu.make_async_remote_copy(
            src_ref=src, dst_ref=dst, send_sem=ss, recv_sem=rs,
            device_id=dev, device_id_type=pl.DeviceIdType.MESH,
        )

    barrier = pltpu.get_barrier_semaphore()
    for dev in (cpeer, xpeer):
        pl.semaphore_signal(barrier, inc=1, device_id=dev, device_id_type=pl.DeviceIdType.MESH)

    @pl.loop(1, n)
    def _(d):
        pl.semaphore_signal(
            barrier, inc=1, device_id={"space": lax.rem(s + d, n)},
            device_id_type=pl.DeviceIdType.MESH,
        )

    @pl.loop(0, mdev * rows)
    def _(i):
        m, row = i // rows, lax.rem(i, rows)
        v = lat_ref[m, row]
        x_ref[1, m, 1 + row] = v
        v = v.astype(F32)
        leo[0, pl.ds(i, 1)] = v[0:1]
        leo[1, pl.ds(i, 1)] = v[cols - 1 : cols]

    pl.semaphore_wait(barrier, n + 1)
    lat_edges = [
        rcopy(leo.at[1], lei.at[0], s_le.at[0], r_le.at[0], right),
        rcopy(leo.at[0], lei.at[1], s_le.at[1], r_le.at[1], left),
    ]
    for c in lat_edges:
        c.start()
    acc[...] = jnp.zeros_like(acc)
    loss_ref[...] = jnp.zeros_like(loss_ref)
    for c in range(3):
        for r in (0, rows + 1):
            sp[c, :, r] = jnp.zeros((mdev, cols, chans), BF16)
            x_ref[c, :, r] = jnp.zeros((mdev, cols, chans), BF16)
    for c in lat_edges:
        c.wait_recv()

    col = lax.broadcasted_iota(jnp.int32, (cols, chans), 0)

    def shift(ref, edge, m, row):
        i = m * rows + row
        v = ref[1, m, 1 + row].astype(F32)
        lo = jnp.where(col == 0, edge[0, pl.ds(i, 1)], pltpu.roll(v, 1, 0))
        hi = jnp.where(col == cols - 1, edge[1, pl.ds(i, 1)], pltpu.roll(v, cols - 1, 0))
        ref[0, m, 1 + row] = lo.astype(BF16)
        ref[2, m, 1 + row] = hi.astype(BF16)

    @pl.loop(0, mdev * rows)
    def _(i):
        shift(x_ref, lei, i // rows, lax.rem(i, rows))


    def to_x(ch):
        return rcopy(own.at[ch], xp.at[ch], s_x.at[ch], r_x.at[ch], xpeer)

    def to_core(ch):
        return rcopy(own.at[ch], co.at[ch], s_c.at[ch], r_c.at[ch], cpeer)

    def relay(ch):
        return rcopy(xp.at[ch], xc.at[ch], s_l.at[ch], r_l.at[ch], cpeer)

    @pl.loop(0, chunks)
    def _(ch):
        total = None
        for a in range(3):
            for b in range(3):
                w = x_ref[b, :, pl.ds(ch * rc + a, rc)].reshape(mdev * cells, chans)
                term = jnp.dot(w, k_ref[a * 3 + b], preferred_element_type=F32)
                total = term if total is None else total + term
        total = total.reshape(mdev, cells, chans)
        f_own[ch] = total
        own[ch] = total.astype(WIRE)
        to_x(ch).start()
        to_core(ch).start()

    def smooth(gap):
        square = gap * gap + smoothing * smoothing
        inv = lax.rsqrt(square)
        return gap * inv, square * inv

    def process(ch):
        @pl.loop(0, rc)
        def _(q):
            row = ch * rc + q
            for blk in range(cols // 16):
                at = pl.ds(pl.multiple_of(q * cols + blk * 16, 16), 16)
                mine = [f_own[ch, m, at] for m in range(mdev)]
                tgt = t_ref[row, pl.ds(blk * 16, 16)].astype(F32)
                slopes, own_w, pair_w = [], None, None
                own_s = []
                for f in mine:
                    sl, w = smooth(f - tgt)
                    own_s.append(sl)
                    own_w = w if own_w is None else own_w + w
                sl, w = smooth(mine[0] - mine[1])
                sums = [sl, -sl]
                pair_w = w + w
                for ref in (co, xp, xc):
                    for m in range(mdev):
                        o = ref[ch, m, at].astype(F32)
                        for k in range(mdev):
                            sl, w = smooth(mine[k] - o)
                            sums[k] = sums[k] + sl
                            pair_w = pair_w + w
                loss_ref[...] += own_w * (1.0 / members) - pair_w * (
                    1.0 / (2 * members * (members - 1))
                )
                for m in range(mdev):
                    sl = own_s[m] * (1.0 / members) - sums[m] * (1.0 / (members * (members - 1)))
                    sp[1, m, 1 + row, pl.ds(blk * 16, 16)] = sl.astype(BF16)
                    if blk == 0:
                        eo[0, pl.ds(m * rows + row, 1)] = sl[0:1]
                    if blk == cols // 16 - 1:
                        eo[1, pl.ds(m * rows + row, 1)] = sl[15:16]

        sl = sp[1, :, pl.ds(1 + ch * rc, rc)].reshape(mdev * cells, chans)
        slt = sl.astype(F32).T.astype(BF16)
        for tap in range(9):
            a, b = tap // 3, tap % 3
            w = x_ref[b, :, pl.ds(ch * rc + a, rc)].reshape(mdev * cells, chans)
            p = jnp.dot(slt, w, preferred_element_type=F32)
            for dh in range(2):
                piece = tap * 2 + dh
                xh, off = piece // 9, (piece % 9) * 128
                for h in range(2):
                    acc[h, xh, off : off + 128] += p[
                        dh * 128 : dh * 128 + 128, h * 128 : h * 128 + 128
                    ]

    to_x(0).wait_recv()
    relay(0).start()

    @pl.loop(0, chunks)
    def _(ch):
        @pl.when(ch + 1 < chunks)
        def _():
            to_x(ch + 1).wait_recv()
            relay(ch + 1).start()

        to_core(ch).wait_recv()
        relay(ch).wait_recv()
        process(ch)

    edges = [
        rcopy(eo.at[1], ei.at[0], s_e.at[0], r_e.at[0], right),
        rcopy(eo.at[0], ei.at[1], s_e.at[1], r_e.at[1], left),
    ]
    for c in edges:
        c.start()

    def span_of(p):
        return pl.ds(p * span, span)

    def part_of(p, i):
        return pl.ds(pl.multiple_of(p * span + i * part, 16), part)

    st_core = {}
    for p in range(PIECES):
        for j in range(2):
            h = 1 - xx if j == 0 else xx
            st_core[p, j] = rcopy(
                acc.at[1 - core, h, span_of(p)], r1.at[h, span_of(p)],
                s_st.at[p, j], r_st.at[p, j], cpeer,
            )
            st_core[p, j].start()
    total = loss_ref[...]
    total = total[0:8, 0:128] + total[8:16, 0:128] + total[0:8, 128:256] + total[8:16, 128:256]
    l1[...] = total
    ls_core = rcopy(l1, lr1, s_ls.at[0], r_ls.at[0], cpeer)
    ls_core.start()

    st_x = []
    for p in range(PIECES):
        st_core[p, 0].wait_recv()
        b2[span_of(p)] = (
            acc[core, 1 - xx, span_of(p)] + r1[1 - xx, span_of(p)]
        ).astype(BF16)
        st_x.append(rcopy(b2.at[span_of(p)], r2.at[span_of(p)], s_x2.at[p], r_x2.at[p], xpeer))
        st_x[p].start()
    ls_core.wait_recv()
    l2[...] = l1[...] + lr1[...]
    ls_x = rcopy(l2, lr2, s_ls.at[1], r_ls.at[1], xpeer)
    ls_x.start()

    for c in edges:
        c.wait_recv()

    @pl.loop(0, mdev * rows)
    def _(i):
        shift(sp, ei, i // rows, lax.rem(i, rows))

    def grad_in(start, stop):
        @pl.loop(start, stop)
        def _(ch):
            total = None
            for a in range(3):
                for b in range(3):
                    w = sp[2 - b, :, pl.ds(ch * rc + 2 - a, rc)].reshape(mdev * cells, chans)
                    term = lax.dot_general(
                        w, k_ref[a * 3 + b], NT, preferred_element_type=F32
                    )
                    total = term if total is None else total + term
            gi_ref[:, pl.ds(ch * rc, rc)] = total.reshape(mdev, rc, cols, chans).astype(BF16)

    def to_strip(p, d, i):
        peer = lax.rem(s + d, n)
        return rcopy(
            b3.at[part_of(p, peer)], r3.at[p, i], s_sp.at[p, d], r_sp.at[p, i], {"space": peer}
        )

    def loss_to_strip(d, i):
        return rcopy(l3, lr3.at[i], s_lp.at[d], r_lp.at[i], {"space": lax.rem(s + d, n)})

    def gather(p, d, i):
        return rcopy(
            gk_ref.at[core, xx, part_of(p, i)], gk_ref.at[core, xx, part_of(p, i)],
            s_ag.at[p, d], r_ag.at[p, i], {"space": lax.rem(s + d, n)},
        )

    marks = [chunks * i // 8 for i in range(9)]
    for p in range(PIECES):
        grad_in(marks[p], marks[p + 1])
        st_core[p, 1].wait_recv()
        st_x[p].wait_recv()
        total = acc[core, xx, span_of(p)] + r1[xx, span_of(p)] + r2[span_of(p)].astype(F32)
        r1[xx, span_of(p)] = total
        b3[span_of(p)] = total.astype(BF16)

        @pl.loop(1, n)
        def _(d):
            to_strip(p, d, s).start()

    ls_x.wait_recv()
    l3[...] = l2[...] + lr2[...]

    @pl.loop(1, n)
    def _(d):
        loss_to_strip(d, s).start()

    for p in range(PIECES):
        grad_in(marks[PIECES + p], marks[PIECES + p + 1])

        def take(d, g):
            peer = lax.rem(s + d, n)
            to_strip(p, d, peer).wait_recv()
            return g + r3[p, peer].astype(F32)

        total = lax.fori_loop(1, n, take, r1[xx, part_of(p, s)])
        gk_ref[core, xx, part_of(p, s)] = total.astype(BF16)

        @pl.loop(1, n)
        def _(d):
            gather(p, d, s).start()

    grad_in(marks[2 * PIECES], chunks)

    def take_loss(d, l):
        peer = lax.rem(s + d, n)
        loss_to_strip(d, peer).wait_recv()
        return l + lr3[peer]

    loss_ref[0:8, 0:128] = lax.fori_loop(1, n, take_loss, l3[...])

    ag_x, ag_c = [], []
    for p in range(PIECES):

        @pl.loop(1, n)
        def _(d):
            gather(p, d, lax.rem(s + d, n)).wait_recv()

        mine = gk_ref.at[core, xx, span_of(p)]
        ag_x.append(rcopy(mine, mine, s_ax.at[p], r_ax.at[p], xpeer))
        ag_x[p].start()
        ag_c.append(rcopy(mine, mine, s_ac.at[p, 0], r_ac.at[p, 0], cpeer))
        ag_c[-1].start()

    for p in range(PIECES):
        theirs = gk_ref.at[core, 1 - xx, span_of(p)]
        rcopy(theirs, theirs, s_ax.at[p], r_ax.at[p], xpeer).wait_recv()
        ag_c.append(rcopy(theirs, theirs, s_ac.at[p, 1], r_ac.at[p, 1], cpeer))
        ag_c[-1].start()

    for p in range(PIECES):
        for j in range(2):
            h = xx if j == 0 else 1 - xx
            theirs = gk_ref.at[1 - core, h, span_of(p)]
            rcopy(theirs, theirs, s_ac.at[p, j], r_ac.at[p, j], cpeer).wait_recv()

    @pl.loop(0, chunks)
    def _(ch):
        to_x(ch).wait_send()
        to_core(ch).wait_send()
        relay(ch).wait_send()

    @pl.loop(1, n)
    def _(d):
        for p in range(PIECES):
            to_strip(p, d, s).wait_send()
            gather(p, d, s).wait_send()
        loss_to_strip(d, s).wait_send()

    for c in lat_edges + edges + list(st_core.values()) + st_x + [ls_core, ls_x] + ag_x + ag_c:
        c.wait_send()


def local(n, latents, targets, kernel):
    mdev, rows, cols, chans = latents.shape
    members = mdev * 4
    chunks = rows // ROW_CHUNK
    cells = ROW_CHUNK * cols
    part = -(-9 * 128 // (16 * n * PIECES)) * 16
    hp = part * n * PIECES
    vmem, dma = pltpu.VMEM, pltpu.SemaphoreType.DMA
    wire = vmem((chunks, mdev, cells, chans), WIRE)
    tile = vmem((8, 128), F32)
    gi, gk, loss = pl.pallas_call(
        functools.partial(body, n, members),
        name="crps_step",
        out_shape=(
            jax.ShapeDtypeStruct(latents.shape, BF16),
            jax.ShapeDtypeStruct((2, 2, hp, 128), BF16),
            jax.ShapeDtypeStruct((16, chans), F32),
        ),
        in_specs=[pl.BlockSpec(memory_space=vmem)] * 3,
        out_specs=(pl.BlockSpec(memory_space=vmem),) * 3,
        scratch_shapes=[
            vmem((3, mdev, rows + 2, cols, chans), BF16),
            vmem((2, mdev * rows, chans), F32),
            vmem((2, mdev * rows, chans), F32),
            vmem((chunks, mdev, cells, chans), F32),
            wire, wire, wire, wire,
            vmem((3, mdev, rows + 2, cols, chans), BF16),
            vmem((2, 2, hp, 128), F32),
            vmem((2, mdev * rows, chans), F32),
            vmem((2, mdev * rows, chans), F32),
            vmem((2, hp, 128), F32),
            vmem((hp, 128), BF16),
            vmem((hp, 128), BF16),
            vmem((hp, 128), BF16),
            vmem((PIECES, n, part, 128), BF16),
            tile, tile, tile, tile, tile,
            vmem((n, 8, 128), F32),
            dma((chunks,)), dma((chunks,)), dma((chunks,)), dma((chunks,)),
            dma((chunks,)), dma((chunks,)),
            dma((2,)), dma((2,)), dma((PIECES, 2)), dma((PIECES, 2)), dma((PIECES,)), dma((PIECES,)),
            dma((2,)), dma((2,)), dma((PIECES, n)), dma((PIECES, n)), dma((n,)), dma((n,)),
            dma((PIECES, n)), dma((PIECES, n)), dma((2,)), dma((2,)),
            dma((PIECES,)), dma((PIECES,)), dma((PIECES, 2)), dma((PIECES, 2)),
        ],
        compiler_params=pltpu.CompilerParams(
            collective_id=0, has_side_effects=True, vmem_limit_bytes=48 * 2**20
        ),
    )(latents, targets, kernel.reshape(9, chans, chans))
    longitude = cols * n
    gk = gk[:, :, : 9 * 128].reshape(2, 9, chans, 128).transpose(1, 0, 3, 2)
    grad_kernel = gk.astype(F32).reshape(3, 3, chans, chans) / (members * rows * longitude)
    loss = jnp.sum(loss[0:8, 0:128]) / (rows * longitude * chans)
    return loss, gi, grad_kernel


def solution(mesh):
    in_specs = (P("ens", None, "space", None), P(None, "space", None), P())
    out_specs = (P(), P("ens", None, "space", None), P())
    return jax.shard_map(
        functools.partial(local, mesh.shape["space"]),
        mesh=mesh, in_specs=in_specs, out_specs=out_specs, check_vma=False,
    )
```

```python
import functools

import jax
import jax.numpy as jnp
from jax import lax
from jax.experimental import pallas as pl
from jax.experimental.pallas import tpu as pltpu
from jax.sharding import PartitionSpec as P

smoothing = 0.1
PIECES = 3
F32, BF16 = jnp.float32, jnp.bfloat16
NT = (((1,), (1,)), ((), ()))


def body(
    n, members,
    lat_ref, t_ref, k_ref,
    gi_ref, gk_ref, loss_ref,
    x_ref, leo, lei, fld, sp, acc, eo, ei, gib, r1, b2, r2, b3, r3, l1, lr1, l2, lr2, l3, lr3,
    s_x, r_x, s_le, r_le, s_e, r_e, s_h, r_h, s_g, r_g,
    s_st, r_st, s_x2, r_x2, s_ls, r_ls, s_sp, r_sp, s_lp, r_lp,
    s_ag, r_ag, s_ax, r_ax, s_ac, r_ac,
):
    mdev, rows, cols, chans = gi_ref.shape
    own_rows = rows // 4
    slots = own_rows + 2
    cells = members * cols
    part = b3.shape[0] // (n * PIECES)
    span = part * n
    e = lax.axis_index("ens")
    s = lax.axis_index("space")
    core = lax.rem(e, 2)
    xx = e // 2
    cpeer = {"ens": xx * 2 + (1 - core)}
    xpeer = {"ens": (1 - xx) * 2 + core}
    right_s = lax.rem(s + 1, n)
    left_s = lax.rem(s + n - 1, n)
    right, left = {"space": right_s}, {"space": left_s}
    MESH = pl.DeviceIdType.MESH

    def rcopy(src, dst, ss, rs, dev):
        return pltpu.make_async_remote_copy(
            src_ref=src, dst_ref=dst, send_sem=ss, recv_sem=rs,
            device_id=dev, device_id_type=MESH,
        )

    def ens_at(d):
        return lax.rem(e + d, 4)

    blank = jnp.zeros((members, cols, chans), BF16)
    for c in range(3):
        for r in (0, slots - 1):
            sp[c, r] = blank
            x_ref[c, r] = blank
    for side in range(2):
        for r in (0, rows + 1):
            leo[side, r] = jnp.zeros((mdev, chans), F32)

    barrier = pltpu.get_barrier_semaphore()
    for d in range(1, 4):
        for strip in (s, right_s, left_s):
            pl.semaphore_signal(
                barrier, inc=1, device_id={"ens": ens_at(d), "space": strip}, device_id_type=MESH
            )

    @pl.loop(1, n)
    def _(d):
        pl.semaphore_signal(
            barrier, inc=1, device_id={"space": lax.rem(s + d, n)}, device_id_type=MESH
        )

    @pl.loop(0, rows)
    def _(row):
        for m in range(mdev):
            v = lat_ref[m, row].astype(F32)
            leo[0, 1 + row, m : m + 1] = v[0:1]
            leo[1, 1 + row, m : m + 1] = v[cols - 1 : cols]

    pl.semaphore_wait(barrier, n - 1 + 9)

    def edge_of(side, d, src):
        to = ens_at(d)
        return rcopy(
            leo.at[side, pl.ds(to * own_rows, slots)], lei.at[1 - side, src],
            s_le.at[side, d], r_le.at[1 - side, src],
            {"ens": to, "space": left_s if side == 0 else right_s},
        )

    for d in (2, 3, 1, 0):
        for side in range(2):
            edge_of(side, d, e).start()

    def row_of(d, to, slot, src):
        row = to * own_rows - 1 + slot
        inside = (row >= 0) & (row < rows)
        return inside, rcopy(
            lat_ref.at[:, jnp.clip(row, 0, rows - 1)], x_ref.at[1, slot, pl.ds(mdev * src, mdev)],
            s_x.at[d, slot], r_x.at[src, slot], {"ens": to},
        )

    @pl.loop(0, slots)
    def _(slot):
        for d in (2, 3, 1):
            inside, c = row_of(d, ens_at(d), slot, e)

            @pl.when(inside)
            def _():
                c.start()

        row = e * own_rows - 1 + slot

        @pl.when((row >= 0) & (row < rows))
        def _():
            for m in range(mdev):
                x_ref[1, slot, e * mdev + m] = lat_ref[m, row]

    acc[...] = jnp.zeros_like(acc)
    loss_ref[...] = jnp.zeros_like(loss_ref)
    for d in (0, 1, 2, 3):
        for side in range(2):
            edge_of(side, d, ens_at(d)).wait_recv()

    col = lax.broadcasted_iota(jnp.int32, (cols, chans), 0)

    def shift(ref, slot, edge):
        for mem in range(members):
            v = ref[1, slot, mem].astype(F32)
            lo = jnp.where(col == 0, edge(0, mem), pltpu.roll(v, 1, 0))
            hi = jnp.where(col == cols - 1, edge(1, mem), pltpu.roll(v, cols - 1, 0))
            ref[0, slot, mem] = lo.astype(BF16)
            ref[2, slot, mem] = hi.astype(BF16)

    def ready(slot):
        for d in range(1, 4):
            inside, c = row_of(d, e, slot, ens_at(d))

            @pl.when(inside)
            def _():
                c.wait_recv()

        shift(
            x_ref, slot,
            lambda side, mem: lei[side, mem // mdev, slot, mem % mdev : mem % mdev + 1],
        )

    def smooth(gap):
        square = gap * gap + smoothing * smoothing
        inv = lax.rsqrt(square)
        return gap * inv, square * inv

    for slot in range(2):
        ready(slot)

    @pl.loop(0, own_rows)
    def _(i):
        ready(i + 2)
        total = None
        for a in range(3):
            for b in range(3):
                w = x_ref[b, i + a].reshape(cells, chans)
                term = jnp.dot(w, k_ref[a * 3 + b], preferred_element_type=F32)
                total = term if total is None else total + term
        fld[...] = total.reshape(members, cols, chans)
        row = e * own_rows + i
        for blk in range(cols // 16):
            for lane in range(chans // 128):
                ln = pl.ds(lane * 128, 128)
                at = pl.ds(blk * 16, 16)
                tgt = t_ref[row, at, ln].astype(F32)
                f = [fld[m, at, ln] for m in range(members)]
                sums = [None] * members
                pair_w = None
                for m in range(members):
                    for o in range(m + 1, members):
                        sl, w = smooth(f[m] - f[o])
                        sums[m] = sl if sums[m] is None else sums[m] + sl
                        sums[o] = -sl if sums[o] is None else sums[o] - sl
                        pair_w = w if pair_w is None else pair_w + w
                own_w = None
                for m in range(members):
                    own_s, w = smooth(f[m] - tgt)
                    own_w = w if own_w is None else own_w + w
                    sl = own_s * (1.0 / members) - sums[m] * (1.0 / (members * (members - 1)))
                    sp[1, 1 + i, m, at, ln] = sl.astype(BF16)
                    if blk == 0:
                        eo[0, i, m : m + 1, ln] = sl[0:1]
                    if blk == cols // 16 - 1:
                        eo[1, i, m : m + 1, ln] = sl[15:16]
                loss_ref[:, ln] += own_w * (1.0 / members) - pair_w * (
                    1.0 / (members * (members - 1))
                )

        slt = sp[1, 1 + i].reshape(cells, chans).astype(F32).T.astype(BF16)
        for tap in range(9):
            a, b = tap // 3, tap % 3
            w = x_ref[b, i + a].reshape(cells, chans)
            p = jnp.dot(slt, w, preferred_element_type=F32)
            for dh in range(2):
                piece = tap * 2 + dh
                xh, off = piece // 9, (piece % 9) * 128
                for h in range(2):
                    acc[h, xh, off : off + 128] += p[
                        dh * 128 : dh * 128 + 128, h * 128 : h * 128 + 128
                    ]

    edges = [
        rcopy(eo.at[1], ei.at[0], s_e.at[0], r_e.at[0], right),
        rcopy(eo.at[0], ei.at[1], s_e.at[1], r_e.at[1], left),
    ]
    for c in edges:
        c.start()

    def span_of(p):
        return pl.ds(p * span, span)

    def part_of(p, i):
        return pl.ds(pl.multiple_of(p * span + i * part, 16), part)

    st_core = {}
    for p in range(PIECES):
        for j in range(2):
            h = 1 - xx if j == 0 else xx
            st_core[p, j] = rcopy(
                acc.at[1 - core, h, span_of(p)], r1.at[h, span_of(p)],
                s_st.at[p, j], r_st.at[p, j], cpeer,
            )
            st_core[p, j].start()
    total = loss_ref[...]
    total = total[0:8, 0:128] + total[8:16, 0:128] + total[0:8, 128:256] + total[8:16, 128:256]
    l1[...] = total
    ls_core = rcopy(l1, lr1, s_ls.at[0], r_ls.at[0], cpeer)
    ls_core.start()

    st_x = []
    for p in range(PIECES):
        st_core[p, 0].wait_recv()
        b2[span_of(p)] = (
            acc[core, 1 - xx, span_of(p)] + r1[1 - xx, span_of(p)]
        ).astype(BF16)
        st_x.append(rcopy(b2.at[span_of(p)], r2.at[span_of(p)], s_x2.at[p], r_x2.at[p], xpeer))
        st_x[p].start()
    ls_core.wait_recv()
    l2[...] = l1[...] + lr1[...]
    ls_x = rcopy(l2, lr2, s_ls.at[1], r_ls.at[1], xpeer)
    ls_x.start()

    for c in edges:
        c.wait_recv()

    @pl.loop(0, own_rows)
    def _(i):
        shift(sp, 1 + i, lambda side, mem: ei[side, i, mem : mem + 1])

    up = rcopy(
        sp.at[:, 1], sp.at[:, slots - 1], s_h.at[0], r_h.at[0], {"ens": jnp.maximum(e - 1, 0)}
    )
    down = rcopy(
        sp.at[:, slots - 2], sp.at[:, 0], s_h.at[1], r_h.at[1], {"ens": jnp.minimum(e + 1, 3)}
    )
    has_up, has_down = e > 0, e < 3

    @pl.when(has_up)
    def _():
        up.start()

    @pl.when(has_down)
    def _():
        down.start()

    def give(i, d, to, src):
        return rcopy(
            gib.at[i, pl.ds(to * mdev, mdev)], gi_ref.at[:, src * own_rows + i],
            s_g.at[d, i], r_g.at[src, i], {"ens": to},
        )

    def grad_in(start, stop):
        @pl.loop(start, stop)
        def _(i):
            total = None
            for a in range(3):
                for b in range(3):
                    w = sp[2 - b, i + 2 - a].reshape(cells, chans)
                    term = lax.dot_general(
                        w, k_ref[a * 3 + b], NT, preferred_element_type=F32
                    )
                    total = term if total is None else total + term
            gib[i] = total.reshape(members, cols, chans).astype(BF16)
            for d in (2, 3, 1):
                give(i, d, ens_at(d), e).start()
            for m in range(mdev):
                gi_ref[m, e * own_rows + i] = gib[i, e * mdev + m]

    def to_strip(p, d, i):
        peer = lax.rem(s + d, n)
        return rcopy(
            b3.at[part_of(p, peer)], r3.at[p, i], s_sp.at[p, d], r_sp.at[p, i], {"space": peer}
        )

    def loss_to_strip(d, i):
        return rcopy(l3, lr3.at[i], s_lp.at[d], r_lp.at[i], {"space": lax.rem(s + d, n)})

    def gather(p, d, i):
        return rcopy(
            gk_ref.at[core, xx, part_of(p, i)], gk_ref.at[core, xx, part_of(p, i)],
            s_ag.at[p, d], r_ag.at[p, i], {"space": lax.rem(s + d, n)},
        )

    marks = [1 + (own_rows - 2) * i // (2 * PIECES) for i in range(2 * PIECES + 1)]
    for p in range(PIECES):
        grad_in(marks[p], marks[p + 1])
        st_core[p, 1].wait_recv()
        st_x[p].wait_recv()
        total = acc[core, xx, span_of(p)] + r1[xx, span_of(p)] + r2[span_of(p)].astype(F32)
        r1[xx, span_of(p)] = total
        b3[span_of(p)] = total.astype(BF16)

        @pl.loop(1, n)
        def _(d):
            to_strip(p, d, s).start()

    ls_x.wait_recv()
    l3[...] = l2[...] + lr2[...]

    @pl.loop(1, n)
    def _(d):
        loss_to_strip(d, s).start()

    for p in range(PIECES):
        grad_in(marks[PIECES + p], marks[PIECES + p + 1])

        def take(d, g):
            peer = lax.rem(s + d, n)
            to_strip(p, d, peer).wait_recv()
            return g + r3[p, peer].astype(F32)

        total = lax.fori_loop(1, n, take, r1[xx, part_of(p, s)])
        gk_ref[core, xx, part_of(p, s)] = total.astype(BF16)

        @pl.loop(1, n)
        def _(d):
            gather(p, d, s).start()

    @pl.when(has_up)
    def _():
        up.wait_send()
        down.wait_recv()

    @pl.when(has_down)
    def _():
        down.wait_send()
        up.wait_recv()

    grad_in(0, 1)
    grad_in(own_rows - 1, own_rows)

    def take_loss(d, l):
        peer = lax.rem(s + d, n)
        loss_to_strip(d, peer).wait_recv()
        return l + lr3[peer]

    loss_ref[0:8, 0:128] = lax.fori_loop(1, n, take_loss, l3[...])

    ag_x, ag_c = [], []
    for p in range(PIECES):

        @pl.loop(1, n)
        def _(d):
            gather(p, d, lax.rem(s + d, n)).wait_recv()

        mine = gk_ref.at[core, xx, span_of(p)]
        ag_x.append(rcopy(mine, mine, s_ax.at[p], r_ax.at[p], xpeer))
        ag_x[p].start()
        ag_c.append(rcopy(mine, mine, s_ac.at[p, 0], r_ac.at[p, 0], cpeer))
        ag_c[-1].start()

    for p in range(PIECES):
        theirs = gk_ref.at[core, 1 - xx, span_of(p)]
        rcopy(theirs, theirs, s_ax.at[p], r_ax.at[p], xpeer).wait_recv()
        ag_c.append(rcopy(theirs, theirs, s_ac.at[p, 1], r_ac.at[p, 1], cpeer))
        ag_c[-1].start()

    for p in range(PIECES):
        for j in range(2):
            h = xx if j == 0 else 1 - xx
            theirs = gk_ref.at[1 - core, h, span_of(p)]
            rcopy(theirs, theirs, s_ac.at[p, j], r_ac.at[p, j], cpeer).wait_recv()

    @pl.loop(0, own_rows)
    def _(i):
        for d in range(1, 4):
            give(i, d, ens_at(d), e).wait_send()
            give(i, d, e, ens_at(d)).wait_recv()

    @pl.loop(0, slots)
    def _(slot):
        for d in range(1, 4):
            inside, c = row_of(d, ens_at(d), slot, e)

            @pl.when(inside)
            def _():
                c.wait_send()

    for d in range(4):
        for side in range(2):
            edge_of(side, d, e).wait_send()

    @pl.loop(1, n)
    def _(d):
        for p in range(PIECES):
            to_strip(p, d, s).wait_send()
            gather(p, d, s).wait_send()
        loss_to_strip(d, s).wait_send()

    for c in edges + list(st_core.values()) + st_x + [ls_core, ls_x] + ag_x + ag_c:
        c.wait_send()


def local(n, latents, targets, kernel):
    mdev, rows, cols, chans = latents.shape
    members = mdev * 4
    own_rows = rows // 4
    slots = own_rows + 2
    part = -(-9 * 128 // (16 * n * PIECES)) * 16
    hp = part * n * PIECES
    vmem, dma = pltpu.VMEM, pltpu.SemaphoreType.DMA
    shifted = vmem((3, slots, members, cols, chans), BF16)
    edge = vmem((2, own_rows, members, chans), F32)
    tile = vmem((8, 128), F32)
    gi, gk, loss = pl.pallas_call(
        functools.partial(body, n, members),
        name="crps_step",
        out_shape=(
            jax.ShapeDtypeStruct(latents.shape, BF16),
            jax.ShapeDtypeStruct((2, 2, hp, 128), BF16),
            jax.ShapeDtypeStruct((16, chans), F32),
        ),
        in_specs=[pl.BlockSpec(memory_space=vmem)] * 3,
        out_specs=(pl.BlockSpec(memory_space=vmem),) * 3,
        scratch_shapes=[
            shifted,
            vmem((2, rows + 2, mdev, chans), F32),
            vmem((2, 4, slots, mdev, chans), F32),
            vmem((members, cols, chans), F32),
            shifted,
            vmem((2, 2, hp, 128), F32),
            edge, edge,
            vmem((own_rows, members, cols, chans), BF16),
            vmem((2, hp, 128), F32),
            vmem((hp, 128), BF16),
            vmem((hp, 128), BF16),
            vmem((hp, 128), BF16),
            vmem((PIECES, n, part, 128), BF16),
            tile, tile, tile, tile, tile,
            vmem((n, 8, 128), F32),
            dma((4, slots)), dma((4, slots)), dma((2, 4)), dma((2, 4)), dma((2,)), dma((2,)),
            dma((2,)), dma((2,)), dma((4, own_rows)), dma((4, own_rows)),
            dma((PIECES, 2)), dma((PIECES, 2)), dma((PIECES,)), dma((PIECES,)),
            dma((2,)), dma((2,)), dma((PIECES, n)), dma((PIECES, n)), dma((n,)), dma((n,)),
            dma((PIECES, n)), dma((PIECES, n)),
            dma((PIECES,)), dma((PIECES,)), dma((PIECES, 2)), dma((PIECES, 2)),
        ],
        compiler_params=pltpu.CompilerParams(
            collective_id=0, has_side_effects=True, vmem_limit_bytes=48 * 2**20
        ),
    )(latents, targets, kernel.reshape(9, chans, chans))
    longitude = cols * n
    gk = gk[:, :, : 9 * 128].reshape(2, 9, chans, 128).transpose(1, 0, 3, 2)
    grad_kernel = gk.astype(F32).reshape(3, 3, chans, chans) / (members * rows * longitude)
    loss = jnp.sum(loss[0:8, 0:128]) / (rows * longitude * chans)
    return loss, gi, grad_kernel


def solution(mesh):
    in_specs = (P("ens", None, "space", None), P(None, "space", None), P())
    out_specs = (P(), P("ens", None, "space", None), P())
    return jax.shard_map(
        functools.partial(local, mesh.shape["space"]),
        mesh=mesh, in_specs=in_specs, out_specs=out_specs, check_vma=False,
    )
```

```python
import functools

import jax
import jax.numpy as jnp
from jax import lax
from jax.experimental import pallas as pl
from jax.experimental.pallas import tpu as pltpu
from jax.sharding import PartitionSpec as P

smoothing = 0.1
PIECES = 3
F32, BF16 = jnp.float32, jnp.bfloat16
NT = (((1,), (1,)), ((), ()))


def body(
    n, members,
    lat_ref, t_ref, k_ref,
    gi_ref, gk_ref, loss_ref,
    x_ref, leo, lei, fld, sp, acc, eo, ei, eh, gib, r1, b2, r2, b3, r3, l1, lr1, l2, lr2, l3, lr3,
    s_x, r_x, s_le, r_le, s_e, r_e, s_h, r_h, s_g, r_g,
    s_st, r_st, s_x2, r_x2, s_ls, r_ls, s_sp, r_sp, s_lp, r_lp,
    s_ag, r_ag, s_ax, r_ax, s_ac, r_ac,
):
    mdev, rows, cols, chans = gi_ref.shape
    own_rows = rows // 4
    slots = own_rows + 2
    cells = members * cols
    part = b3.shape[0] // (n * PIECES)
    span = part * n
    e = lax.axis_index("ens")
    s = lax.axis_index("space")
    core = lax.rem(e, 2)
    xx = e // 2
    cpeer = {"ens": xx * 2 + (1 - core)}
    xpeer = {"ens": (1 - xx) * 2 + core}
    right_s = lax.rem(s + 1, n)
    left_s = lax.rem(s + n - 1, n)
    right, left = {"space": right_s}, {"space": left_s}
    MESH = pl.DeviceIdType.MESH

    def rcopy(src, dst, ss, rs, dev):
        return pltpu.make_async_remote_copy(
            src_ref=src, dst_ref=dst, send_sem=ss, recv_sem=rs,
            device_id=dev, device_id_type=MESH,
        )

    def ens_at(d):
        return lax.rem(e + d, 4)

    blank = jnp.zeros((members, cols, chans), BF16)
    for c in range(3):
        for r in (0, slots - 1):
            sp[c, r] = blank
            x_ref[c, r] = blank
    for side in range(2):
        for r in (0, rows + 1):
            leo[side, r] = jnp.zeros((mdev, chans), F32)

    barrier = pltpu.get_barrier_semaphore()
    for d in range(1, 4):
        for strip in (s, right_s, left_s):
            pl.semaphore_signal(
                barrier, inc=1, device_id={"ens": ens_at(d), "space": strip}, device_id_type=MESH
            )

    @pl.loop(1, n)
    def _(d):
        pl.semaphore_signal(
            barrier, inc=1, device_id={"space": lax.rem(s + d, n)}, device_id_type=MESH
        )

    @pl.loop(0, rows)
    def _(row):
        for m in range(mdev):
            v = lat_ref[m, row].astype(F32)
            leo[0, 1 + row, m : m + 1] = v[0:1]
            leo[1, 1 + row, m : m + 1] = v[cols - 1 : cols]

    pl.semaphore_wait(barrier, n - 1 + 9)

    def edge_of(side, d, src):
        to = ens_at(d)
        return rcopy(
            leo.at[side, pl.ds(to * own_rows, slots)], lei.at[1 - side, src],
            s_le.at[side, d], r_le.at[1 - side, src],
            {"ens": to, "space": left_s if side == 0 else right_s},
        )

    for d in (2, 3, 1, 0):
        for side in range(2):
            edge_of(side, d, e).start()

    def row_of(d, to, slot, src):
        row = to * own_rows - 1 + slot
        inside = (row >= 0) & (row < rows)
        return inside, rcopy(
            lat_ref.at[:, jnp.clip(row, 0, rows - 1)], x_ref.at[1, slot, pl.ds(mdev * src, mdev)],
            s_x.at[d, slot], r_x.at[src, slot], {"ens": to},
        )

    @pl.loop(0, slots)
    def _(slot):
        for d in (2, 3, 1):
            inside, c = row_of(d, ens_at(d), slot, e)

            @pl.when(inside)
            def _():
                c.start()

        row = e * own_rows - 1 + slot

        @pl.when((row >= 0) & (row < rows))
        def _():
            for m in range(mdev):
                x_ref[1, slot, e * mdev + m] = lat_ref[m, row]

    acc[...] = jnp.zeros_like(acc)
    loss_ref[...] = jnp.zeros_like(loss_ref)
    for d in (0, 1, 2, 3):
        for side in range(2):
            edge_of(side, d, ens_at(d)).wait_recv()

    col = lax.broadcasted_iota(jnp.int32, (cols, chans), 0)

    def shift(ref, slot, edge):
        for mem in range(members):
            v = ref[1, slot, mem].astype(F32)
            lo = jnp.where(col == 0, edge(0, mem), pltpu.roll(v, 1, 0))
            hi = jnp.where(col == cols - 1, edge(1, mem), pltpu.roll(v, cols - 1, 0))
            ref[0, slot, mem] = lo.astype(BF16)
            ref[2, slot, mem] = hi.astype(BF16)

    def ready(slot):
        for d in range(1, 4):
            inside, c = row_of(d, e, slot, ens_at(d))

            @pl.when(inside)
            def _():
                c.wait_recv()

        shift(
            x_ref, slot,
            lambda side, mem: lei[side, mem // mdev, slot, mem % mdev : mem % mdev + 1],
        )

    def smooth(gap):
        square = gap * gap + smoothing * smoothing
        inv = lax.rsqrt(square)
        return gap * inv, square * inv

    for slot in range(2):
        ready(slot)

    @pl.loop(0, own_rows)
    def _(i):
        ready(i + 2)
        total = None
        for a in range(3):
            for b in range(3):
                w = x_ref[b, i + a].reshape(cells, chans)
                term = jnp.dot(w, k_ref[a * 3 + b], preferred_element_type=F32)
                total = term if total is None else total + term
        fld[...] = total.reshape(members, cols, chans)
        row = e * own_rows + i
        for blk in range(cols // 16):
            for lane in range(chans // 128):
                ln = pl.ds(lane * 128, 128)
                at = pl.ds(blk * 16, 16)
                tgt = t_ref[row, at, ln].astype(F32)
                f = [fld[m, at, ln] for m in range(members)]
                sums = [None] * members
                pair_w = None
                for m in range(members):
                    for o in range(m + 1, members):
                        sl, w = smooth(f[m] - f[o])
                        sums[m] = sl if sums[m] is None else sums[m] + sl
                        sums[o] = -sl if sums[o] is None else sums[o] - sl
                        pair_w = w if pair_w is None else pair_w + w
                own_w = None
                for m in range(members):
                    own_s, w = smooth(f[m] - tgt)
                    own_w = w if own_w is None else own_w + w
                    sl = own_s * (1.0 / members) - sums[m] * (1.0 / (members * (members - 1)))
                    sp[1, 1 + i, m, at, ln] = sl.astype(BF16)
                    if blk == 0:
                        eo[0, i, m : m + 1, ln] = sl[0:1]
                    if blk == cols // 16 - 1:
                        eo[1, i, m : m + 1, ln] = sl[15:16]
                loss_ref[:, ln] += own_w * (1.0 / members) - pair_w * (
                    1.0 / (members * (members - 1))
                )

        slt = sp[1, 1 + i].reshape(cells, chans).astype(F32).T.astype(BF16)
        for tap in range(9):
            a, b = tap // 3, tap % 3
            w = x_ref[b, i + a].reshape(cells, chans)
            p = jnp.dot(slt, w, preferred_element_type=F32)
            for dh in range(2):
                piece = tap * 2 + dh
                xh, off = piece // 9, (piece % 9) * 128
                for h in range(2):
                    acc[h, xh, off : off + 128] += p[
                        dh * 128 : dh * 128 + 128, h * 128 : h * 128 + 128
                    ]

    edges = [
        rcopy(eo.at[1], ei.at[0], s_e.at[0], r_e.at[0], right),
        rcopy(eo.at[0], ei.at[1], s_e.at[1], r_e.at[1], left),
    ]
    for c in edges:
        c.start()

    def span_of(p):
        return pl.ds(p * span, span)

    def part_of(p, i):
        return pl.ds(pl.multiple_of(p * span + i * part, 16), part)

    st_core = {}
    for p in range(PIECES):
        for j in range(2):
            h = 1 - xx if j == 0 else xx
            st_core[p, j] = rcopy(
                acc.at[1 - core, h, span_of(p)], r1.at[h, span_of(p)],
                s_st.at[p, j], r_st.at[p, j], cpeer,
            )
            st_core[p, j].start()
    total = loss_ref[...]
    total = total[0:8, 0:128] + total[8:16, 0:128] + total[0:8, 128:256] + total[8:16, 128:256]
    l1[...] = total
    ls_core = rcopy(l1, lr1, s_ls.at[0], r_ls.at[0], cpeer)
    ls_core.start()

    st_x = []
    for p in range(PIECES):
        st_core[p, 0].wait_recv()
        b2[span_of(p)] = (
            acc[core, 1 - xx, span_of(p)] + r1[1 - xx, span_of(p)]
        ).astype(BF16)
        st_x.append(rcopy(b2.at[span_of(p)], r2.at[span_of(p)], s_x2.at[p], r_x2.at[p], xpeer))
        st_x[p].start()
    ls_core.wait_recv()
    l2[...] = l1[...] + lr1[...]
    ls_x = rcopy(l2, lr2, s_ls.at[1], r_ls.at[1], xpeer)
    ls_x.start()

    for c in edges:
        c.wait_recv()

    @pl.loop(0, own_rows)
    def _(i):
        shift(sp, 1 + i, lambda side, mem: ei[side, i, mem : mem + 1])

    above, below = {"ens": jnp.maximum(e - 1, 0)}, {"ens": jnp.minimum(e + 1, 3)}
    up = (
        rcopy(sp.at[1, 1], sp.at[1, slots - 1], s_h.at[0], r_h.at[0], above),
        rcopy(ei.at[:, 0], eh.at[1], s_h.at[2], r_h.at[2], above),
    )
    down = (
        rcopy(sp.at[1, slots - 2], sp.at[1, 0], s_h.at[1], r_h.at[1], below),
        rcopy(ei.at[:, own_rows - 1], eh.at[0], s_h.at[3], r_h.at[3], below),
    )
    has_up, has_down = e > 0, e < 3

    @pl.when(has_up)
    def _():
        for c in up:
            c.start()

    @pl.when(has_down)
    def _():
        for c in down:
            c.start()

    def give(i, d, to, src):
        return rcopy(
            gib.at[i, pl.ds(to * mdev, mdev)], gi_ref.at[:, src * own_rows + i],
            s_g.at[d, i], r_g.at[src, i], {"ens": to},
        )

    def grad_in(start, stop):
        @pl.loop(start, stop)
        def _(i):
            total = None
            for a in range(3):
                for b in range(3):
                    w = sp[2 - b, i + 2 - a].reshape(cells, chans)
                    term = lax.dot_general(
                        w, k_ref[a * 3 + b], NT, preferred_element_type=F32
                    )
                    total = term if total is None else total + term
            gib[i] = total.reshape(members, cols, chans).astype(BF16)
            for d in (2, 3, 1):
                give(i, d, ens_at(d), e).start()
            for m in range(mdev):
                gi_ref[m, e * own_rows + i] = gib[i, e * mdev + m]

    def to_strip(p, d, i):
        peer = lax.rem(s + d, n)
        return rcopy(
            b3.at[part_of(p, peer)], r3.at[p, i], s_sp.at[p, d], r_sp.at[p, i], {"space": peer}
        )

    def loss_to_strip(d, i):
        return rcopy(l3, lr3.at[i], s_lp.at[d], r_lp.at[i], {"space": lax.rem(s + d, n)})

    def gather(p, d, i):
        return rcopy(
            gk_ref.at[core, xx, part_of(p, i)], gk_ref.at[core, xx, part_of(p, i)],
            s_ag.at[p, d], r_ag.at[p, i], {"space": lax.rem(s + d, n)},
        )

    marks = [1 + (own_rows - 2) * i // (2 * PIECES) for i in range(2 * PIECES + 1)]
    for p in range(PIECES):
        grad_in(marks[p], marks[p + 1])
        st_core[p, 1].wait_recv()
        st_x[p].wait_recv()
        total = acc[core, xx, span_of(p)] + r1[xx, span_of(p)] + r2[span_of(p)].astype(F32)
        r1[xx, span_of(p)] = total
        b3[span_of(p)] = total.astype(BF16)

        @pl.loop(1, n)
        def _(d):
            to_strip(p, d, s).start()

    ls_x.wait_recv()
    l3[...] = l2[...] + lr2[...]

    @pl.loop(1, n)
    def _(d):
        loss_to_strip(d, s).start()

    for p in range(PIECES):
        grad_in(marks[PIECES + p], marks[PIECES + p + 1])

        def take(d, g):
            peer = lax.rem(s + d, n)
            to_strip(p, d, peer).wait_recv()
            return g + r3[p, peer].astype(F32)

        total = lax.fori_loop(1, n, take, r1[xx, part_of(p, s)])
        gk_ref[core, xx, part_of(p, s)] = total.astype(BF16)

        @pl.loop(1, n)
        def _(d):
            gather(p, d, s).start()

    @pl.when(has_up)
    def _():
        for c in up:
            c.wait_send()
        for c in down:
            c.wait_recv()
        shift(sp, 0, lambda side, mem: eh[0, side, mem : mem + 1])

    @pl.when(has_down)
    def _():
        for c in down:
            c.wait_send()
        for c in up:
            c.wait_recv()
        shift(sp, slots - 1, lambda side, mem: eh[1, side, mem : mem + 1])

    grad_in(0, 1)
    grad_in(own_rows - 1, own_rows)

    def take_loss(d, l):
        peer = lax.rem(s + d, n)
        loss_to_strip(d, peer).wait_recv()
        return l + lr3[peer]

    loss_ref[0:8, 0:128] = lax.fori_loop(1, n, take_loss, l3[...])

    ag_x, ag_c = [], []
    for p in range(PIECES):

        @pl.loop(1, n)
        def _(d):
            gather(p, d, lax.rem(s + d, n)).wait_recv()

        mine = gk_ref.at[core, xx, span_of(p)]
        ag_x.append(rcopy(mine, mine, s_ax.at[p], r_ax.at[p], xpeer))
        ag_x[p].start()
        ag_c.append(rcopy(mine, mine, s_ac.at[p, 0], r_ac.at[p, 0], cpeer))
        ag_c[-1].start()

    for p in range(PIECES):
        theirs = gk_ref.at[core, 1 - xx, span_of(p)]
        rcopy(theirs, theirs, s_ax.at[p], r_ax.at[p], xpeer).wait_recv()
        ag_c.append(rcopy(theirs, theirs, s_ac.at[p, 1], r_ac.at[p, 1], cpeer))
        ag_c[-1].start()

    for p in range(PIECES):
        for j in range(2):
            h = xx if j == 0 else 1 - xx
            theirs = gk_ref.at[1 - core, h, span_of(p)]
            rcopy(theirs, theirs, s_ac.at[p, j], r_ac.at[p, j], cpeer).wait_recv()

    @pl.loop(0, own_rows)
    def _(i):
        for d in range(1, 4):
            give(i, d, ens_at(d), e).wait_send()
            give(i, d, e, ens_at(d)).wait_recv()

    @pl.loop(0, slots)
    def _(slot):
        for d in range(1, 4):
            inside, c = row_of(d, ens_at(d), slot, e)

            @pl.when(inside)
            def _():
                c.wait_send()

    for d in range(4):
        for side in range(2):
            edge_of(side, d, e).wait_send()

    @pl.loop(1, n)
    def _(d):
        for p in range(PIECES):
            to_strip(p, d, s).wait_send()
            gather(p, d, s).wait_send()
        loss_to_strip(d, s).wait_send()

    for c in edges + list(st_core.values()) + st_x + [ls_core, ls_x] + ag_x + ag_c:
        c.wait_send()


def local(n, latents, targets, kernel):
    mdev, rows, cols, chans = latents.shape
    members = mdev * 4
    own_rows = rows // 4
    slots = own_rows + 2
    part = -(-9 * 128 // (16 * n * PIECES)) * 16
    hp = part * n * PIECES
    vmem, dma = pltpu.VMEM, pltpu.SemaphoreType.DMA
    shifted = vmem((3, slots, members, cols, chans), BF16)
    edge = vmem((2, own_rows, members, chans), F32)
    tile = vmem((8, 128), F32)
    gi, gk, loss = pl.pallas_call(
        functools.partial(body, n, members),
        name="crps_step",
        out_shape=(
            jax.ShapeDtypeStruct(latents.shape, BF16),
            jax.ShapeDtypeStruct((2, 2, hp, 128), BF16),
            jax.ShapeDtypeStruct((16, chans), F32),
        ),
        in_specs=[pl.BlockSpec(memory_space=vmem)] * 3,
        out_specs=(pl.BlockSpec(memory_space=vmem),) * 3,
        scratch_shapes=[
            shifted,
            vmem((2, rows + 2, mdev, chans), F32),
            vmem((2, 4, slots, mdev, chans), F32),
            vmem((members, cols, chans), F32),
            shifted,
            vmem((2, 2, hp, 128), F32),
            edge, edge,
            vmem((2, 2, members, chans), F32),
            vmem((own_rows, members, cols, chans), BF16),
            vmem((2, hp, 128), F32),
            vmem((hp, 128), BF16),
            vmem((hp, 128), BF16),
            vmem((hp, 128), BF16),
            vmem((PIECES, n, part, 128), BF16),
            tile, tile, tile, tile, tile,
            vmem((n, 8, 128), F32),
            dma((4, slots)), dma((4, slots)), dma((2, 4)), dma((2, 4)), dma((2,)), dma((2,)),
            dma((4,)), dma((4,)), dma((4, own_rows)), dma((4, own_rows)),
            dma((PIECES, 2)), dma((PIECES, 2)), dma((PIECES,)), dma((PIECES,)),
            dma((2,)), dma((2,)), dma((PIECES, n)), dma((PIECES, n)), dma((n,)), dma((n,)),
            dma((PIECES, n)), dma((PIECES, n)),
            dma((PIECES,)), dma((PIECES,)), dma((PIECES, 2)), dma((PIECES, 2)),
        ],
        compiler_params=pltpu.CompilerParams(
            collective_id=0, has_side_effects=True, vmem_limit_bytes=48 * 2**20
        ),
    )(latents, targets, kernel.reshape(9, chans, chans))
    longitude = cols * n
    gk = gk[:, :, : 9 * 128].reshape(2, 9, chans, 128).transpose(1, 0, 3, 2)
    grad_kernel = gk.astype(F32).reshape(3, 3, chans, chans) / (members * rows * longitude)
    loss = jnp.sum(loss[0:8, 0:128]) / (rows * longitude * chans)
    return loss, gi, grad_kernel


def solution(mesh):
    in_specs = (P("ens", None, "space", None), P(None, "space", None), P())
    out_specs = (P(), P("ens", None, "space", None), P())
    return jax.shard_map(
        functools.partial(local, mesh.shape["space"]),
        mesh=mesh, in_specs=in_specs, out_specs=out_specs, check_vma=False,
    )
```
